32 devices in a mesh: grp: 8 (over z, y), col: 4 (over x, core).
Axes of the slice: x: 2, y: 2, z: 4, core: 2. Of those that a mesh axis runs over, the one named last changes fastest.
Arguments:
- right_side: float32 [256, 64, 128], P('grp', 'col'), may hold values from -6 to 6
- conductance: float32 [256, 64, 128], P('grp', 'col'), may hold values from 0.3 to 3
- reaction: float32 [256, 64, 128], P('grp', 'col'), may hold values from 0.05 to 0.5
- geneo: bfloat16 [6, 256, 64, 128], P(None, 'grp', 'col'), may hold values from -0.0234375 to 0.0234375
- coarse_inverse: float32 [8, 24, 24], P('grp'), as said below
Outputs:
- solution: float32 [256, 64, 128], P('grp', 'col')
- residual: float32 [256, 64, 128], P('grp', 'col')
The draws below stay inside these ranges and needn't reach their ends.
Inputs may be any that keep to these rules, and one draw needn't show every extreme that they name: `coarse_inverse`: for each first-dimension block, a dense matrix of order 24.
All inputs are finite; a program needn't handle non-finite values.
Results may differ from the reference program's by a relative error of at most 0.0003.
Values sent between devices are 32-bit elements; how exact they have to be, the bound alone decides.
A program may use at most 64 MiB of HBM per device.

```python
import math
import jax
import jax.numpy as jnp
from jax import lax

CX = 32
CY = 16
CZ = 128
NC = 6
OV = 2
SWEEPS = 3
NX = 256
NY = 64
NZ = 128
NCS = 24
N_GRP = 8
N_COL = 4


def draw_coarse_inverse(key, part):
    key_base, key_diag, key_pair, key_spike = jax.random.split(jax.random.fold_in(key, 7), 4)
    blocks = N_COL
    base = jax.random.normal(key_base, (N_GRP, NCS, NCS), jnp.float32) * (0.5 / NCS ** 0.5)
    diag_values = jax.random.uniform(key_diag, (N_GRP, NCS), jnp.float32, 0.5, 1.5)
    pair_keys = jax.random.split(key_pair, N_GRP)
    pairing = jax.vmap(lambda one_key: jax.random.permutation(one_key, blocks))(pair_keys)
    row_block = jnp.arange(NCS, dtype=jnp.int32) // NC
    col_block = jnp.arange(NCS, dtype=jnp.int32) // NC
    partner = pairing[:, row_block]
    spike_mask = (col_block[None, None, :] == partner[:, :, None]).astype(jnp.float32)
    spike = spike_mask * jax.random.normal(key_spike, (N_GRP, NCS, NCS), jnp.float32) * (0.5 / NC ** 0.5)
    index = jnp.arange(NCS, dtype=jnp.int32)
    eye_part = (index[:, None] == index[None, :]).astype(jnp.float32)[None, :, :] * diag_values[:, :, None]
    return 64.0 * (base + spike + eye_part)


def levels(rng, extent, cuts, low, top_value):
    loudness = 1.0
    for axis_at, blocks in cuts:
        steps = jax.random.uniform(jax.random.fold_in(jax.random.fold_in(rng, 6), axis_at), (blocks,), jnp.float32, low / len(cuts), top_value / len(cuts))
        loudness = loudness * jnp.repeat(jnp.exp(steps), extent[axis_at] // blocks).reshape((-1,) + (1,) * (len(extent) - 1 - axis_at))
    return loudness


def normal_values(key, dims, deviation, bound, cuts=(), kind=jnp.bfloat16):
    drawn = jax.random.normal(key, dims, jnp.float32) * deviation
    if len(cuts) > 0:
        drawn = levels(key, dims, cuts, -0.22, 0.18) * drawn
    return jnp.clip(drawn, min=-bound, max=bound).astype(kind)


def setup_inputs(seed: int = 0) -> dict:
    splits = jax.random.split(jax.random.key(seed), 6)
    return {
        "right_side": normal_values(splits[0], (NX, NY, NZ), 1.0, 6.0, ((0, 8), (1, 4)), jnp.float32),
        "conductance": jnp.clip(jnp.exp(math.log(3.0) - 2.3025851 * jax.random.uniform(splits[1], (NX, NY, NZ), jnp.float32) ** levels(splits[1], (NX, NY, NZ), ((0, 8), (1, 4)), -0.2, 0.2)), 0.3, 3.0),
        "reaction": jnp.clip(jnp.exp(math.log(0.5) - 2.3025851 * jax.random.uniform(splits[2], (NX, NY, NZ), jnp.float32) ** levels(splits[2], (NX, NY, NZ), ((0, 8), (1, 4)), -0.2, 0.2)), 0.05, 0.5),
        "geneo": normal_values(splits[3], (NC, NX, NY, NZ), (CX * CY * CZ) ** -0.5, 0.0234375, ((1, 8), (2, 4))),
        "coarse_inverse": draw_coarse_inverse(jax.random.fold_in(splits[5], 71), 0),
    }


highest = lax.Precision.HIGHEST

def face_terms(k_rim, s_mid):
    centre = k_rim[1:-1, 1:-1]
    k_depth = jnp.pad(centre, ((0, 0), (0, 0), (1, 1)))
    west = 0.5 * (centre + k_rim[:-2, 1:-1])
    east = 0.5 * (centre + k_rim[2:, 1:-1])
    south = 0.5 * (centre + k_rim[1:-1, :-2])
    north = 0.5 * (centre + k_rim[1:-1, 2:])
    below = 0.5 * (centre + k_depth[:, :, :-2])
    above = 0.5 * (centre + k_depth[:, :, 2:])
    diagonal = s_mid + west + east + south + north + below + above
    return (west, east, south, north, below, above, diagonal)

def apply_faces(terms, padded):
    west, east, south, north, below, above, diagonal = terms
    middle = padded[1:-1, 1:-1]
    depth = jnp.pad(middle, ((0, 0), (0, 0), (1, 1)))
    beside_all = west * padded[:-2, 1:-1] + east * padded[2:, 1:-1]
    beside_all = beside_all + south * padded[1:-1, :-2] + north * padded[1:-1, 2:]
    beside_all = beside_all + below * depth[:, :, :-2] + above * depth[:, :, 2:]
    return diagonal * middle - beside_all

def local_solve(terms, inside, source):
    inverse = inside / jnp.where(inside > 0, terms[6], 1.0)
    guess = jnp.zeros_like(source)
    for sweep in range(SWEEPS):
        padded = jnp.pad(guess, ((1, 1), (1, 1), (0, 0)))
        guess = guess + inverse * (source - apply_faces(terms, padded))
    return guess

def reference(right_side, conductance, reaction, geneo, coarse_inverse):
    k_pad = jnp.pad(conductance, ((1, 1), (1, 1), (0, 0)))

    def operator(field):
        terms = face_terms(k_pad, reaction)
        return apply_faces(terms, jnp.pad(field, ((1, 1), (1, 1), (0, 0))))
    k_big = jnp.pad(conductance, ((OV + 1, OV + 1), (OV + 1, OV + 1), (0, 0)))
    s_big = jnp.pad(reaction, ((OV, OV), (OV, OV), (0, 0)))
    vectors = geneo.astype(jnp.float32).reshape(NC, N_GRP, CX, N_COL, CY, CZ)

    def precondition(field):
        v_big = jnp.pad(field, ((OV, OV), (OV, OV), (0, 0)))

        def one_block(index):
            block_x = (index // N_COL).astype(jnp.int32)
            block_y = (index % N_COL).astype(jnp.int32)
            x_start = block_x * CX
            y_start = block_y * CY
            zero = jnp.zeros((), jnp.int32)
            k_rim = lax.dynamic_slice(k_big, (x_start, y_start, zero), (CX + 2 * OV + 2, CY + 2 * OV + 2, CZ))
            s_mid = lax.dynamic_slice(s_big, (x_start, y_start, zero), (CX + 2 * OV, CY + 2 * OV, CZ))
            source = lax.dynamic_slice(v_big, (x_start, y_start, zero), (CX + 2 * OV, CY + 2 * OV, CZ))
            x_index = x_start - OV + jnp.arange(CX + 2 * OV, dtype=jnp.int32)
            y_index = y_start - OV + jnp.arange(CY + 2 * OV, dtype=jnp.int32)
            x_valid = ((x_index >= 0) & (x_index < NX)).astype(jnp.float32)
            y_valid = ((y_index >= 0) & (y_index < NY)).astype(jnp.float32)
            inside = x_valid[:, None, None] * y_valid[None, :, None] * jnp.ones((1, 1, CZ), jnp.float32)
            solved = local_solve(face_terms(k_rim, s_mid), inside, source)
            return solved[OV:OV + CX, OV:OV + CY]
        blocks = lax.map(one_block, jnp.arange(N_GRP * N_COL, dtype=jnp.int32))
        local_part = blocks.reshape(N_GRP, N_COL, CX, CY, CZ).transpose(0, 2, 1, 3, 4).reshape(NX, NY, NZ)
        shaped = field.reshape(N_GRP, CX, N_COL, CY, CZ)
        restricted = jnp.einsum('kaxbyz,axbyz->abk', vectors, shaped, precision=highest).reshape(N_GRP, NCS)
        coarse = jnp.einsum('aij,aj->ai', coarse_inverse, restricted, precision=highest).reshape(N_GRP, N_COL, NC)
        correction = jnp.einsum('kaxbyz,abk->axbyz', vectors, coarse, precision=highest).reshape(NX, NY, NZ)
        return local_part + correction
    z_raw = precondition(right_side)
    w_raw = operator(z_raw)
    bb = jnp.sum(right_side * right_side)
    bw = jnp.sum(right_side * w_raw)
    beta = jnp.sqrt(bb)
    h11 = bw / bb
    first = right_side / beta
    z_one = z_raw / beta
    w_one = (w_raw - h11 * right_side) / beta
    h21 = jnp.sqrt(jnp.sum(w_one * w_one))
    second = w_one / h21
    z_two = precondition(second)
    w_two = operator(z_two)
    h12 = jnp.sum(first * w_two)
    h22 = jnp.sum(second * w_two)
    rest = w_two - h12 * first - h22 * second
    h32 = jnp.sqrt(jnp.sum(rest * rest))
    third = rest / h32
    g11 = h11 * h11 + h21 * h21
    g12 = h11 * h12 + h21 * h22
    g22 = h12 * h12 + h22 * h22 + h32 * h32
    rhs_one = beta * h11
    rhs_two = beta * h12
    determinant = g11 * g22 - g12 * g12
    y_one = (g22 * rhs_one - g12 * rhs_two) / determinant
    y_two = (g11 * rhs_two - g12 * rhs_one) / determinant
    solution = y_one * z_one + y_two * z_two
    left_one = beta - h11 * y_one - h12 * y_two
    left_two = -h21 * y_one - h22 * y_two
    left_three = -h32 * y_two
    residual = left_one * first + left_two * second + left_three * third
    return (solution, residual)
```

```python
import functools

import jax
import jax.numpy as jnp
from jax import lax
from jax.experimental import pallas as pl
from jax.experimental.pallas import tpu as pltpu
from jax.sharding import PartitionSpec as P

F32 = jnp.float32
MESH = pl.DeviceIdType.MESH
G = 3
T2 = 16
ROWS = 24


def loop(lo, hi, step, body, init=()):
    count = (hi - lo) // step

    def several(i, carry):
        for j in range(step):
            carry = body(lo + i * step + j, carry)
        return carry

    carry = lax.fori_loop(0, count, several, init)
    for x in range(lo + count * step, hi):
        carry = body(x, carry)
    return carry


def kernel(
    n_p, n_q, b_hbm, k_hbm, s_hbm, g_hbm, m_hbm, sol_hbm, res_hbm,
    K, S, B, Z1, Z2, W, U, V, EX, NY, SY, AZ, BZ, INV, D, Y2,
    geneo, minv, face_lo, face_hi, edge_p, edge_m,
    zs1, zr1, zs2, zr2, ws, wr, cs, cr,
    rc_out, rc1, rc2, c_scr, row_out, ar1, ar2, sol, res,
    load_sem, send_sem, recv_sem, all_sem,
):
    p = lax.axis_index("grp")
    q = lax.axis_index("col")
    nx = k_hbm.shape[0]
    nc = geneo.shape[0]
    ncs = minv.shape[1]
    n_all = n_p * n_q
    me = p * n_q + q
    last = G + nx
    own = pl.ds(G, nx)
    low = pl.ds(0, T2)
    f = slice(None)

    loads = []
    for i, (src, dst) in enumerate((
        (k_hbm, K.at[own, low]), (s_hbm, S.at[own, low]), (b_hbm, B.at[own, low]),
        (g_hbm, geneo), (m_hbm, minv),
    )):
        copy = pltpu.make_async_copy(src, dst, load_sem.at[i])
        copy.start()
        loads.append(copy)

    barrier = pltpu.get_barrier_semaphore()

    def other(t):
        dest = lax.rem(me + t, n_all)
        return (lax.div(dest, n_q), lax.rem(dest, n_q))

    def greet(t, carry):
        pl.semaphore_signal(barrier, inc=1, device_id=other(t), device_id_type=MESH)
        return carry

    lax.fori_loop(1, n_all, greet, 0)

    lane = lax.broadcasted_iota(jnp.int32, (1, 128), 1)
    sub = lax.broadcasted_iota(jnp.int32, (8, 128), 0)
    row = lax.broadcasted_iota(jnp.int32, (ROWS, 128), 0)

    counter = [0]

    def transfer(src, dst, dp, dq):
        i = counter[0]
        counter[0] += 1
        to_p, to_q = p + dp, q + dq
        from_p, from_q = p - dp, q - dq
        sends = (to_p >= 0) & (to_p < n_p) & (to_q >= 0) & (to_q < n_q)
        takes = (from_p >= 0) & (from_p < n_p) & (from_q >= 0) & (from_q < n_q)
        copy = pltpu.make_async_remote_copy(
            src_ref=src, dst_ref=dst, send_sem=send_sem.at[i], recv_sem=recv_sem.at[i],
            device_id=(to_p, to_q), device_id_type=MESH,
        )
        return copy, sends, takes, dst

    pending = []

    def start(items):
        for copy, sends, takes, dst in items:
            pl.when(sends)(copy.start)
            pending.append((copy, sends))

    def arrive(items):
        for copy, sends, takes, dst in items:
            pl.when(takes)(copy.wait_recv)

    def blank(items):
        for copy, sends, takes, dst in items:
            @pl.when(jnp.logical_not(takes))
            def _():
                dst[...] = jnp.zeros(dst.shape, F32)

    r1 = []
    for array, src, width in ((K, k_hbm, 3), (S, s_hbm, 2), (B, b_hbm, 2)):
        r1.append(transfer(src.at[pl.ds(nx - width, width)], array.at[pl.ds(G - width, width), low], 1, 0))
        r1.append(transfer(src.at[pl.ds(0, width)], array.at[pl.ds(last, width), low], -1, 0))
    r1.append(transfer(face_hi, edge_m.at[own], 0, 1))
    r1.append(transfer(face_lo, edge_p.at[own], 0, -1))
    for dp, here, there in ((1, pl.ds(nx - G, G), pl.ds(0, G)), (-1, pl.ds(0, G), pl.ds(last, G))):
        r1.append(transfer(face_hi.at[here], edge_m.at[there], dp, 1))
        r1.append(transfer(face_lo.at[here], edge_p.at[there], dp, -1))

    def z_round(Z, zs, zr):
        return [
            transfer(Z.at[last - 1, low], Z.at[G - 1, low], 1, 0),
            transfer(Z.at[G, low], Z.at[last, low], -1, 0),
            transfer(zs.at[1], zr.at[1], 0, 1),
            transfer(zs.at[0], zr.at[0], 0, -1),
        ]

    r2 = z_round(Z1, zs1, zr1)
    r4 = z_round(Z2, zs2, zr2)
    r3 = [
        transfer(W.at[pl.ds(last - 2, 2), low], W.at[pl.ds(G - 2, 2), low], 1, 0),
        transfer(W.at[pl.ds(G, 2), low], W.at[pl.ds(last, 2), low], -1, 0),
        transfer(ws.at[1], wr.at[1], 0, 1),
        transfer(ws.at[0], wr.at[0], 0, -1),
        transfer(cs.at[0], cr.at[0], 1, 1),
        transfer(cs.at[1], cr.at[1], 1, -1),
        transfer(cs.at[2], cr.at[2], -1, 1),
        transfer(cs.at[3], cr.at[3], -1, -1),
    ]
    for items in (r1, r2, r3, r4):
        blank(items)

    def spread(src, dst, i, devices):
        count, slot, where = devices

        def one(t):
            return pltpu.make_async_remote_copy(
                src_ref=src, dst_ref=dst.at[slot], send_sem=all_sem.at[2 * i], recv_sem=all_sem.at[2 * i + 1],
                device_id=where(t), device_id_type=MESH,
            )

        def go(t, carry):
            one(t).start()
            return carry

        lax.fori_loop(1, count, go, 0)
        dst[slot] = src[...]

        def whole():
            part = dst.at[pl.ds(0, count - 1)]
            return pltpu.make_async_remote_copy(
                src_ref=part, dst_ref=part, send_sem=all_sem.at[2 * i], recv_sem=all_sem.at[2 * i + 1],
                device_id=where(1), device_id_type=MESH,
            )

        return whole

    in_col = (n_q, q, lambda t: (p, lax.rem(q + t, n_q)))
    in_all = (n_all, me, other)

    def packed(parts, first_lane):
        tile = jnp.zeros((8, 128), F32)
        for i, part in enumerate(parts):
            tile = jnp.where(sub == i, jnp.sum(part, axis=0, keepdims=True), tile)
        sums = jnp.sum(tile, axis=1, keepdims=True)
        lanes = lax.broadcasted_iota(jnp.int32, (8, 128), 1)
        placed = jnp.where(lanes == sub + first_lane, sums, 0.0)
        return jnp.sum(jnp.where(sub < len(parts), placed, 0.0), axis=0, keepdims=True)

    def restrict(src):
        def step(x, carry):
            value = src[x, low]
            return tuple(acc + geneo[j, x - G].astype(F32) * value for j, acc in enumerate(carry))

        sums = loop(G, last, 2, step, tuple(jnp.zeros((T2, 128), F32) for _ in range(nc)))
        return packed(sums, q * nc)

    def coarse(rc):
        total = rc[0]
        for i in range(1, n_q):
            total = total + rc[i]
        c = jnp.sum(minv[0] * total[:, :ncs], axis=1, keepdims=True)
        c_scr[...] = jnp.broadcast_to(c, (ncs, 128))
        return [c_scr[pl.ds(q * nc + j, 1), :] for j in range(nc)]

    for copy in loads[:3]:
        copy.wait()

    def pack(x, carry):
        kl, sl, bl = K[x, 0:8], S[x, 0:8], B[x, 0:8]
        kt, st, bt = K[x, 8:16], S[x, 8:16], B[x, 8:16]
        face_lo[x - G] = jnp.where(sub < 3, kl, jnp.where(sub < 5, pltpu.roll(sl, 3, 0), pltpu.roll(bl, 5, 0)))
        face_hi[x - G] = jnp.where(sub > 4, kt, jnp.where(sub > 2, pltpu.roll(st, 5, 0), pltpu.roll(bt, 3, 0)))
        return carry

    loop(G, last, 4, pack)
    pl.semaphore_wait(barrier, n_all - 1)
    start(r1)
    loads[3].wait()
    loads[4].wait()
    rc_out[0] = restrict(B)
    rc_wait1 = spread(rc_out.at[0], rc1, 0, in_col)
    arrive(r1)

    def fill(x, carry):
        plus, minus = edge_p[x], edge_m[x]
        K[x, 16:24] = jnp.where(sub < 4, plus, minus)
        S[x, 16:24] = jnp.where(sub < 4, pltpu.roll(plus, 5, 0), pltpu.roll(minus, 3, 0))
        B[x, 16:24] = jnp.where(sub < 4, pltpu.roll(plus, 3, 0), pltpu.roll(minus, 5, 0))
        return carry

    loop(0, last + G, 2, fill)
    y_ok = (row < T2) | ((row < T2 + 2) & (q < n_q - 1)) | ((row >= ROWS - 2) & (q > 0))

    EX[0] = 0.5 * (K[0] + K[1])

    def terms(x, carry):
        kh = 0.5 * K[x]
        east = kh + 0.5 * K[x + 1]
        EX[x] = east
        north = kh + pltpu.roll(kh, ROWS - 1, 0)
        south = kh + pltpu.roll(kh, 1, 0)
        above = jnp.where(lane < 127, pltpu.roll(kh, 127, 1), 0.0)
        below = jnp.where(lane > 0, pltpu.roll(kh, 1, 1), 0.0)
        d = S[x] + east + EX[x - 1] + north + south + ((kh + above) + (kh + below))
        x_ok = ((x >= G) | (p > 0)) & ((x < last) | (p < n_p - 1))
        inv = jnp.where(y_ok & x_ok, 1.0 / d, 0.0)
        NY[x] = north
        SY[x] = south
        AZ[x] = jnp.where(lane < 127, kh + above, 0.0)
        BZ[x] = jnp.where(lane > 0, kh + below, 0.0)
        D[x] = d
        INV[x] = inv
        U[x] = inv * B[x]
        return carry

    loop(1, last + 2, 2, terms)

    def beside(A, x, r):
        mid = A[x]
        total = EX[x - 1, r] * A[x - 1, r] + EX[x, r] * A[x + 1, r]
        total = total + NY[x, r] * pltpu.roll(mid, ROWS - 1, 0)[r] + SY[x, r] * pltpu.roll(mid, 1, 0)[r]
        part = mid[r]
        return total + AZ[x, r] * pltpu.roll(part, 127, 1) + BZ[x, r] * pltpu.roll(part, 1, 1)

    every = slice(0, ROWS)
    mine = slice(0, T2)

    def solve(src, dst, rc, zs):
        def second(x, carry):
            V[x] = INV[x] * (src[x] + beside(U, x, every))
            return carry

        loop(G - 1, last + 1, 2, second)
        c = coarse(rc)

        def third(x, carry):
            value = INV[x, mine] * (src[x, mine] + beside(V, x, mine))
            for j in range(nc):
                value = value + c[j] * geneo[j, x - G].astype(F32)
            dst[x, mine] = value
            zs[0, pl.ds(x - G, 1)] = value[0:1]
            zs[1, pl.ds(x - G, 1)] = value[15:16]
            return carry

        loop(G, last, 2, third)

    def margin_one(Z, zr):
        def put(x, carry):
            Z[x, 16:24] = jnp.where(sub == 0, zr[0, pl.ds(x - G, 1)], jnp.where(sub == 7, zr[1, pl.ds(x - G, 1)], 0.0))
            return carry

        loop(G, last, 4, put)

    rc_wait1().wait_recv()
    solve(B, Z1, rc1, zs1)
    start(r2)
    arrive(r2)
    margin_one(Z1, zr1)

    zero = jnp.zeros((T2, 128), F32)

    def image_one(x, carry):
        bb, bw, ww = carry
        w = D[x, mine] * Z1[x, mine] - beside(Z1, x, mine)
        b = B[x, mine]
        W[x, mine] = w
        i = x - G
        ws[0, pl.ds(i, 1)] = w[0:1]
        ws[0, pl.ds(nx + i, 1)] = w[1:2]
        ws[1, pl.ds(i, 1)] = w[15:16]
        ws[1, pl.ds(nx + i, 1)] = w[14:15]
        return bb + b * b, bw + b * w, ww + w * w

    bb_part, bw_part, ww_part = loop(G, last, 2, image_one, (zero, zero, zero))
    for i, (x, r) in enumerate(((last - 1, 15), (last - 1, 0), (G, 15), (G, 0))):
        cs[i] = jnp.broadcast_to(W[x, r : r + 1], (8, 128))
    start(r3)
    rc_out[1] = restrict(W)
    rc_wait2 = spread(rc_out.at[1], rc2, 1, in_col)
    row_out[0] = packed((bb_part, bw_part, ww_part), 0)
    ar_wait1 = spread(row_out.at[0], ar1, 2, in_all)
    arrive(r3)

    def put_w(x, carry):
        i = x - G
        tile = jnp.where(sub == 0, wr[0, pl.ds(i, 1)], jnp.where(sub == 1, wr[0, pl.ds(nx + i, 1)], 0.0))
        tile = jnp.where(sub == 7, wr[1, pl.ds(i, 1)], jnp.where(sub == 6, wr[1, pl.ds(nx + i, 1)], tile))
        W[x, 16:24] = tile
        return carry

    loop(G, last, 2, put_w)
    blank_tile = jnp.zeros((8, 128), F32)
    W[G - 2, 16:24] = blank_tile
    W[last + 1, 16:24] = blank_tile
    W[G - 1, 16:24] = jnp.where(sub == 7, cr[0], jnp.where(sub == 0, cr[1], 0.0))
    W[last, 16:24] = jnp.where(sub == 7, cr[2], jnp.where(sub == 0, cr[3], 0.0))

    def first_sweep(x, carry):
        U[x] = INV[x] * W[x]
        return carry

    loop(G - 2, last + 2, 2, first_sweep)
    rc_wait2().wait_recv()
    solve(W, Z2, rc2, zs2)
    start(r4)

    def totals(ar):
        if n_all <= 64:
            total = ar[0]
            for i in range(1, n_all):
                total = total + ar[i]
        else:
            total = lax.fori_loop(1, n_all, lambda i, acc: acc + ar[i], ar[0])
        return [jnp.sum(jnp.where(lane == i, total, 0.0), axis=1, keepdims=True) for i in range(3)]

    ar_wait1().wait_recv()
    bb, bw, ww = totals(ar1)
    h = bw / bb
    arrive(r4)
    margin_one(Z2, zr2)

    def image_two(x, carry):
        wq, qq, bq = carry
        w = W[x, mine]
        image = D[x, mine] * Z2[x, mine] - beside(Z2, x, mine) - h * w
        Y2[x - G] = image
        return wq + w * image, qq + image * image, bq + B[x, mine] * image

    wq_part, qq_part, bq_part = loop(G, last, 2, image_two, (zero, zero, zero))
    row_out[1] = packed((wq_part, qq_part, bq_part), 0)
    ar_wait2 = spread(row_out.at[1], ar2, 3, in_all)
    ar_wait2().wait_recv()
    wq, qq, bq = totals(ar2)
    g11, g12, g22 = ww / bb, wq / bb, qq / bb
    rhs_one, rhs_two = h, bq / bb
    determinant = g11 * g22 - g12 * g12
    y_one = (g22 * rhs_one - g12 * rhs_two) / determinant
    y_two = (g11 * rhs_two - g12 * rhs_one) / determinant
    y_mix = y_one - y_two * h

    def finish(x, carry):
        sol[x - G] = y_mix * Z1[x, mine] + y_two * Z2[x, mine]
        res[x - G] = B[x, mine] - y_one * W[x, mine] - y_two * Y2[x - G]
        return carry

    loop(G, last, 4, finish)
    outs = []
    for i, (src, dst) in enumerate(((sol, sol_hbm), (res, res_hbm))):
        copy = pltpu.make_async_copy(src, dst, load_sem.at[5 + i])
        copy.start()
        outs.append(copy)
    for copy, sends in pending:
        pl.when(sends)(copy.wait_send)
    for wait in (rc_wait1, rc_wait2, ar_wait1, ar_wait2):
        wait().wait_send()
    for copy in outs:
        copy.wait()


def body(n_p, n_q, right_side, conductance, reaction, geneo, coarse_inverse):
    nx, ny, nz = right_side.shape
    assert ny == T2 and nz == 128
    nc = geneo.shape[0]
    ncs = coarse_inverse.shape[1]
    n_all = n_p * n_q
    region = pltpu.VMEM((nx + 2 * G, ROWS, nz), F32)
    field = pltpu.VMEM((nx, ny, nz), F32)
    scratch = [region] * 15 + [
        field,
        pltpu.VMEM(geneo.shape, geneo.dtype),
        pltpu.VMEM(coarse_inverse.shape, F32),
        pltpu.VMEM((nx, 8, nz), F32), pltpu.VMEM((nx, 8, nz), F32),
        pltpu.VMEM((nx + 2 * G, 8, nz), F32), pltpu.VMEM((nx + 2 * G, 8, nz), F32),
    ]
    scratch += [pltpu.VMEM((2, nx, nz), F32)] * 4
    scratch += [pltpu.VMEM((2, 2 * nx, nz), F32)] * 2
    scratch += [pltpu.VMEM((4, 8, nz), F32)] * 2
    scratch += [
        pltpu.VMEM((2, 1, nz), F32), pltpu.VMEM((n_q, 1, nz), F32), pltpu.VMEM((n_q, 1, nz), F32),
        pltpu.VMEM((ncs, nz), F32),
        pltpu.VMEM((2, 1, nz), F32), pltpu.VMEM((n_all, 1, nz), F32), pltpu.VMEM((n_all, 1, nz), F32),
        field, field,
        pltpu.SemaphoreType.DMA((7,)),
        pltpu.SemaphoreType.DMA((28,)), pltpu.SemaphoreType.DMA((28,)),
        pltpu.SemaphoreType.DMA((8,)),
    ]
    out = jax.ShapeDtypeStruct(right_side.shape, F32)
    return pl.pallas_call(
        functools.partial(kernel, n_p, n_q),
        out_shape=(out, out),
        in_specs=[pl.BlockSpec(memory_space=pl.ANY)] * 5,
        out_specs=(pl.BlockSpec(memory_space=pl.ANY),) * 2,
        scratch_shapes=scratch,
        compiler_params=pltpu.CompilerParams(collective_id=0, has_side_effects=True, vmem_limit_bytes=40 * 2**20),
    )(right_side, conductance, reaction, geneo, coarse_inverse)


def solution(mesh):
    return jax.shard_map(
        functools.partial(body, mesh.shape["grp"], mesh.shape["col"]),
        mesh=mesh,
        in_specs=(
            P("grp", "col", None),
            P("grp", "col", None),
            P("grp", "col", None),
            P(None, "grp", "col", None),
            P("grp", None, None),
        ),
        out_specs=(P("grp", "col", None), P("grp", "col", None)),
        check_vma=False,
    )
```

```python
import functools

import jax
import jax.numpy as jnp
from jax import lax
from jax.experimental import pallas as pl
from jax.experimental.pallas import tpu as pltpu
from jax.sharding import PartitionSpec as P

F32 = jnp.float32
MESH = pl.DeviceIdType.MESH
G = 3
T2 = 16
ROWS = 24


def loop(lo, hi, step, body, init=()):
    count = (hi - lo) // step

    def several(i, carry):
        for j in range(step):
            carry = body(lo + i * step + j, carry)
        return carry

    carry = lax.fori_loop(0, count, several, init)
    for x in range(lo + count * step, hi):
        carry = body(x, carry)
    return carry


def kernel(
    n_p, n_q, b_hbm, k_hbm, s_hbm, g_hbm, m_hbm, sol_hbm, res_hbm,
    K, S, B, Z1, Z2, W, U, V, EX, NY, SY, AZ, BZ, INV, D, Y2,
    geneo, minv, face_lo, face_hi, edge_p, edge_m,
    zs1, zr1, zs2, zr2, ws, wr, cs, cr,
    rc_out, rc1, rc2, c_scr, row_out, ar1, ar2, sol, res,
    load_sem, send_sem, recv_sem, all_sem,
):
    p = lax.axis_index("grp")
    q = lax.axis_index("col")
    nx = k_hbm.shape[0]
    nc = geneo.shape[0]
    ncs = minv.shape[1]
    n_all = n_p * n_q
    me = p * n_q + q
    last = G + nx
    own = pl.ds(G, nx)
    low = pl.ds(0, T2)
    f = slice(None)

    loads = []
    for i, (src, dst) in enumerate((
        (k_hbm, K.at[own, low]), (s_hbm, S.at[own, low]), (b_hbm, B.at[own, low]),
        (g_hbm, geneo), (m_hbm, minv),
    )):
        copy = pltpu.make_async_copy(src, dst, load_sem.at[i])
        copy.start()
        loads.append(copy)

    barrier = pltpu.get_barrier_semaphore()

    def other(t):
        dest = lax.rem(me + t, n_all)
        return (lax.div(dest, n_q), lax.rem(dest, n_q))

    def greet(t, carry):
        pl.semaphore_signal(barrier, inc=1, device_id=other(t), device_id_type=MESH)
        return carry

    lax.fori_loop(1, n_all, greet, 0)

    lane = lax.broadcasted_iota(jnp.int32, (1, 128), 1)
    sub = lax.broadcasted_iota(jnp.int32, (8, 128), 0)
    row = lax.broadcasted_iota(jnp.int32, (ROWS, 128), 0)

    counter = [0]

    def transfer(src, dst, dp, dq):
        i = counter[0]
        counter[0] += 1
        to_p, to_q = p + dp, q + dq
        from_p, from_q = p - dp, q - dq
        sends = (to_p >= 0) & (to_p < n_p) & (to_q >= 0) & (to_q < n_q)
        takes = (from_p >= 0) & (from_p < n_p) & (from_q >= 0) & (from_q < n_q)
        copy = pltpu.make_async_remote_copy(
            src_ref=src, dst_ref=dst, send_sem=send_sem.at[i], recv_sem=recv_sem.at[i],
            device_id=(to_p, to_q), device_id_type=MESH,
        )
        return copy, sends, takes, dst

    pending = []

    def start(items):
        for copy, sends, takes, dst in items:
            pl.when(sends)(copy.start)
            pending.append((copy, sends))

    def arrive(items):
        for copy, sends, takes, dst in items:
            pl.when(takes)(copy.wait_recv)

    def blank(items):
        for copy, sends, takes, dst in items:
            @pl.when(jnp.logical_not(takes))
            def _():
                dst[...] = jnp.zeros(dst.shape, F32)

    r1 = []
    for array, src, width in ((K, k_hbm, 3), (S, s_hbm, 2), (B, b_hbm, 2)):
        r1.append(transfer(src.at[pl.ds(nx - width, width)], array.at[pl.ds(G - width, width), low], 1, 0))
        r1.append(transfer(src.at[pl.ds(0, width)], array.at[pl.ds(last, width), low], -1, 0))
    r1.append(transfer(face_hi, edge_m.at[own], 0, 1))
    r1.append(transfer(face_lo, edge_p.at[own], 0, -1))
    for dp, here, there in ((1, pl.ds(nx - G, G), pl.ds(0, G)), (-1, pl.ds(0, G), pl.ds(last, G))):
        r1.append(transfer(face_hi.at[here], edge_m.at[there], dp, 1))
        r1.append(transfer(face_lo.at[here], edge_p.at[there], dp, -1))

    def z_round(Z, zs, zr):
        return [
            transfer(Z.at[last - 1, low], Z.at[G - 1, low], 1, 0),
            transfer(Z.at[G, low], Z.at[last, low], -1, 0),
            transfer(zs.at[1], zr.at[1], 0, 1),
            transfer(zs.at[0], zr.at[0], 0, -1),
        ]

    r2 = z_round(Z1, zs1, zr1)
    r4 = z_round(Z2, zs2, zr2)
    r3 = [
        transfer(W.at[pl.ds(last - 2, 2), low], W.at[pl.ds(G - 2, 2), low], 1, 0),
        transfer(W.at[pl.ds(G, 2), low], W.at[pl.ds(last, 2), low], -1, 0),
        transfer(ws.at[1], wr.at[1], 0, 1),
        transfer(ws.at[0], wr.at[0], 0, -1),
        transfer(cs.at[0], cr.at[0], 1, 1),
        transfer(cs.at[1], cr.at[1], 1, -1),
        transfer(cs.at[2], cr.at[2], -1, 1),
        transfer(cs.at[3], cr.at[3], -1, -1),
    ]
    for items in (r1, r2, r3, r4):
        blank(items)

    def spread(src, dst, i, devices):
        count, slot, where = devices

        def one(t):
            return pltpu.make_async_remote_copy(
                src_ref=src, dst_ref=dst.at[slot], send_sem=all_sem.at[2 * i], recv_sem=all_sem.at[2 * i + 1],
                device_id=where(t), device_id_type=MESH,
            )

        def go(t, carry):
            one(t).start()
            return carry

        lax.fori_loop(1, count, go, 0)
        dst[slot] = src[...]

        def whole():
            part = dst.at[pl.ds(0, count - 1)]
            return pltpu.make_async_remote_copy(
                src_ref=part, dst_ref=part, send_sem=all_sem.at[2 * i], recv_sem=all_sem.at[2 * i + 1],
                device_id=where(1), device_id_type=MESH,
            )

        return whole

    in_col = (n_q, q, lambda t: (p, lax.rem(q + t, n_q)))
    in_all = (n_all, me, other)

    def packed(parts, first_lane):
        tile = jnp.zeros((8, 128), F32)
        for i, part in enumerate(parts):
            tile = jnp.where(sub == i, jnp.sum(part, axis=0, keepdims=True), tile)
        sums = jnp.sum(tile, axis=1, keepdims=True)
        lanes = lax.broadcasted_iota(jnp.int32, (8, 128), 1)
        placed = jnp.where(lanes == sub + first_lane, sums, 0.0)
        return jnp.sum(jnp.where(sub < len(parts), placed, 0.0), axis=0, keepdims=True)

    def restrict(src):
        def step(x, carry):
            value = src[x, low]
            return tuple(acc + geneo[j, x - G].astype(F32) * value for j, acc in enumerate(carry))

        sums = loop(G, last, 16, step, tuple(jnp.zeros((T2, 128), F32) for _ in range(nc)))
        return packed(sums, q * nc)

    def coarse(rc):
        total = rc[0]
        for i in range(1, n_q):
            total = total + rc[i]
        c = jnp.sum(minv[0] * total[:, :ncs], axis=1, keepdims=True)
        c_scr[...] = jnp.broadcast_to(c, (ncs, 128))
        return [c_scr[pl.ds(q * nc + j, 1), :] for j in range(nc)]

    for copy in loads[:3]:
        copy.wait()

    def pack(x, carry):
        kl, sl, bl = K[x, 0:8], S[x, 0:8], B[x, 0:8]
        kt, st, bt = K[x, 8:16], S[x, 8:16], B[x, 8:16]
        face_lo[x - G] = jnp.where(sub < 3, kl, jnp.where(sub < 5, pltpu.roll(sl, 3, 0), pltpu.roll(bl, 5, 0)))
        face_hi[x - G] = jnp.where(sub > 4, kt, jnp.where(sub > 2, pltpu.roll(st, 5, 0), pltpu.roll(bt, 3, 0)))
        return carry

    loop(G, last, 4, pack)
    pl.semaphore_wait(barrier, n_all - 1)
    start(r1)
    loads[3].wait()
    loads[4].wait()
    rc_out[0] = restrict(B)
    rc_wait1 = spread(rc_out.at[0], rc1, 0, in_col)
    arrive(r1)

    def fill(x, carry):
        plus, minus = edge_p[x], edge_m[x]
        K[x, 16:24] = jnp.where(sub < 4, plus, minus)
        S[x, 16:24] = jnp.where(sub < 4, pltpu.roll(plus, 5, 0), pltpu.roll(minus, 3, 0))
        B[x, 16:24] = jnp.where(sub < 4, pltpu.roll(plus, 3, 0), pltpu.roll(minus, 5, 0))
        return carry

    loop(0, last + G, 16, fill)
    y_ok = (row < T2) | ((row < T2 + 2) & (q < n_q - 1)) | ((row >= ROWS - 2) & (q > 0))

    EX[0] = 0.5 * (K[0] + K[1])

    def terms(x, carry):
        kh = 0.5 * K[x]
        east = kh + 0.5 * K[x + 1]
        EX[x] = east
        north = kh + pltpu.roll(kh, ROWS - 1, 0)
        south = kh + pltpu.roll(kh, 1, 0)
        above = jnp.where(lane < 127, pltpu.roll(kh, 127, 1), 0.0)
        below = jnp.where(lane > 0, pltpu.roll(kh, 1, 1), 0.0)
        d = S[x] + east + EX[x - 1] + north + south + ((kh + above) + (kh + below))
        x_ok = ((x >= G) | (p > 0)) & ((x < last) | (p < n_p - 1))
        inv = jnp.where(y_ok & x_ok, 1.0 / d, 0.0)
        NY[x] = north
        SY[x] = south
        AZ[x] = jnp.where(lane < 127, kh + above, 0.0)
        BZ[x] = jnp.where(lane > 0, kh + below, 0.0)
        D[x] = d
        INV[x] = inv
        U[x] = inv * B[x]
        return carry

    loop(1, last + 2, 16, terms)

    def beside(A, x, r):
        mid = A[x]
        total = EX[x - 1, r] * A[x - 1, r] + EX[x, r] * A[x + 1, r]
        total = total + NY[x, r] * pltpu.roll(mid, ROWS - 1, 0)[r] + SY[x, r] * pltpu.roll(mid, 1, 0)[r]
        part = mid[r]
        return total + AZ[x, r] * pltpu.roll(part, 127, 1) + BZ[x, r] * pltpu.roll(part, 1, 1)

    every = slice(0, ROWS)
    mine = slice(0, T2)

    def solve(src, dst, rc, zs):
        def second(x, carry):
            V[x] = INV[x] * (src[x] + beside(U, x, every))
            return carry

        loop(G - 1, last + 1, 16, second)
        c = coarse(rc)

        def third(x, carry):
            value = INV[x, mine] * (src[x, mine] + beside(V, x, mine))
            for j in range(nc):
                value = value + c[j] * geneo[j, x - G].astype(F32)
            dst[x, mine] = value
            zs[0, pl.ds(x - G, 1)] = value[0:1]
            zs[1, pl.ds(x - G, 1)] = value[15:16]
            return carry

        loop(G, last, 16, third)

    def margin_one(Z, zr):
        def put(x, carry):
            Z[x, 16:24] = jnp.where(sub == 0, zr[0, pl.ds(x - G, 1)], jnp.where(sub == 7, zr[1, pl.ds(x - G, 1)], 0.0))
            return carry

        loop(G, last, 4, put)

    rc_wait1().wait_recv()
    solve(B, Z1, rc1, zs1)
    start(r2)
    arrive(r2)
    margin_one(Z1, zr1)

    zero = jnp.zeros((T2, 128), F32)

    def image_one(x, carry):
        bb, bw, ww = carry
        w = D[x, mine] * Z1[x, mine] - beside(Z1, x, mine)
        b = B[x, mine]
        W[x, mine] = w
        i = x - G
        ws[0, pl.ds(i, 1)] = w[0:1]
        ws[0, pl.ds(nx + i, 1)] = w[1:2]
        ws[1, pl.ds(i, 1)] = w[15:16]
        ws[1, pl.ds(nx + i, 1)] = w[14:15]
        return bb + b * b, bw + b * w, ww + w * w

    bb_part, bw_part, ww_part = loop(G, last, 16, image_one, (zero, zero, zero))
    for i, (x, r) in enumerate(((last - 1, 15), (last - 1, 0), (G, 15), (G, 0))):
        cs[i] = jnp.broadcast_to(W[x, r : r + 1], (8, 128))
    start(r3)
    rc_out[1] = restrict(W)
    rc_wait2 = spread(rc_out.at[1], rc2, 1, in_col)
    row_out[0] = packed((bb_part, bw_part, ww_part), 0)
    ar_wait1 = spread(row_out.at[0], ar1, 2, in_all)
    arrive(r3)

    def put_w(x, carry):
        i = x - G
        tile = jnp.where(sub == 0, wr[0, pl.ds(i, 1)], jnp.where(sub == 1, wr[0, pl.ds(nx + i, 1)], 0.0))
        tile = jnp.where(sub == 7, wr[1, pl.ds(i, 1)], jnp.where(sub == 6, wr[1, pl.ds(nx + i, 1)], tile))
        W[x, 16:24] = tile
        return carry

    loop(G, last, 16, put_w)
    blank_tile = jnp.zeros((8, 128), F32)
    W[G - 2, 16:24] = blank_tile
    W[last + 1, 16:24] = blank_tile
    W[G - 1, 16:24] = jnp.where(sub == 7, cr[0], jnp.where(sub == 0, cr[1], 0.0))
    W[last, 16:24] = jnp.where(sub == 7, cr[2], jnp.where(sub == 0, cr[3], 0.0))

    def first_sweep(x, carry):
        U[x] = INV[x] * W[x]
        return carry

    loop(G - 2, last + 2, 16, first_sweep)
    rc_wait2().wait_recv()
    solve(W, Z2, rc2, zs2)
    start(r4)

    def totals(ar):
        if n_all <= 64:
            total = ar[0]
            for i in range(1, n_all):
                total = total + ar[i]
        else:
            total = lax.fori_loop(1, n_all, lambda i, acc: acc + ar[i], ar[0])
        return [jnp.sum(jnp.where(lane == i, total, 0.0), axis=1, keepdims=True) for i in range(3)]

    ar_wait1().wait_recv()
    bb, bw, ww = totals(ar1)
    h = bw / bb
    arrive(r4)
    margin_one(Z2, zr2)

    def image_two(x, carry):
        wq, qq, bq = carry
        w = W[x, mine]
        image = D[x, mine] * Z2[x, mine] - beside(Z2, x, mine) - h * w
        Y2[x - G] = image
        return wq + w * image, qq + image * image, bq + B[x, mine] * image

    wq_part, qq_part, bq_part = loop(G, last, 16, image_two, (zero, zero, zero))
    row_out[1] = packed((wq_part, qq_part, bq_part), 0)
    ar_wait2 = spread(row_out.at[1], ar2, 3, in_all)
    ar_wait2().wait_recv()
    wq, qq, bq = totals(ar2)
    g11, g12, g22 = ww / bb, wq / bb, qq / bb
    rhs_one, rhs_two = h, bq / bb
    determinant = g11 * g22 - g12 * g12
    y_one = (g22 * rhs_one - g12 * rhs_two) / determinant
    y_two = (g11 * rhs_two - g12 * rhs_one) / determinant
    y_mix = y_one - y_two * h

    def finish(x, carry):
        sol[x - G] = y_mix * Z1[x, mine] + y_two * Z2[x, mine]
        res[x - G] = B[x, mine] - y_one * W[x, mine] - y_two * Y2[x - G]
        return carry

    loop(G, last, 4, finish)
    outs = []
    for i, (src, dst) in enumerate(((sol, sol_hbm), (res, res_hbm))):
        copy = pltpu.make_async_copy(src, dst, load_sem.at[5 + i])
        copy.start()
        outs.append(copy)
    for copy, sends in pending:
        pl.when(sends)(copy.wait_send)
    for wait in (rc_wait1, rc_wait2, ar_wait1, ar_wait2):
        wait().wait_send()
    for copy in outs:
        copy.wait()


def body(n_p, n_q, right_side, conductance, reaction, geneo, coarse_inverse):
    nx, ny, nz = right_side.shape
    assert ny == T2 and nz == 128
    nc = geneo.shape[0]
    ncs = coarse_inverse.shape[1]
    n_all = n_p * n_q
    region = pltpu.VMEM((nx + 2 * G, ROWS, nz), F32)
    field = pltpu.VMEM((nx, ny, nz), F32)
    scratch = [region] * 15 + [
        field,
        pltpu.VMEM(geneo.shape, geneo.dtype),
        pltpu.VMEM(coarse_inverse.shape, F32),
        pltpu.VMEM((nx, 8, nz), F32), pltpu.VMEM((nx, 8, nz), F32),
        pltpu.VMEM((nx + 2 * G, 8, nz), F32), pltpu.VMEM((nx + 2 * G, 8, nz), F32),
    ]
    scratch += [pltpu.VMEM((2, nx, nz), F32)] * 4
    scratch += [pltpu.VMEM((2, 2 * nx, nz), F32)] * 2
    scratch += [pltpu.VMEM((4, 8, nz), F32)] * 2
    scratch += [
        pltpu.VMEM((2, 1, nz), F32), pltpu.VMEM((n_q, 1, nz), F32), pltpu.VMEM((n_q, 1, nz), F32),
        pltpu.VMEM((ncs, nz), F32),
        pltpu.VMEM((2, 1, nz), F32), pltpu.VMEM((n_all, 1, nz), F32), pltpu.VMEM((n_all, 1, nz), F32),
        field, field,
        pltpu.SemaphoreType.DMA((7,)),
        pltpu.SemaphoreType.DMA((28,)), pltpu.SemaphoreType.DMA((28,)),
        pltpu.SemaphoreType.DMA((8,)),
    ]
    out = jax.ShapeDtypeStruct(right_side.shape, F32)
    return pl.pallas_call(
        functools.partial(kernel, n_p, n_q),
        out_shape=(out, out),
        in_specs=[pl.BlockSpec(memory_space=pl.ANY)] * 5,
        out_specs=(pl.BlockSpec(memory_space=pl.ANY),) * 2,
        scratch_shapes=scratch,
        compiler_params=pltpu.CompilerParams(collective_id=0, has_side_effects=True, vmem_limit_bytes=67043328),
    )(right_side, conductance, reaction, geneo, coarse_inverse)


def solution(mesh):
    return jax.shard_map(
        functools.partial(body, mesh.shape["grp"], mesh.shape["col"]),
        mesh=mesh,
        in_specs=(
            P("grp", "col", None),
            P("grp", "col", None),
            P("grp", "col", None),
            P(None, "grp", "col", None),
            P("grp", None, None),
        ),
        out_specs=(P("grp", "col", None), P("grp", "col", None)),
        check_vma=False,
    )
```

```python
import functools

import jax
import jax.numpy as jnp
from jax import lax
from jax.experimental import pallas as pl
from jax.experimental.pallas import tpu as pltpu
from jax.sharding import PartitionSpec as P

F32 = jnp.float32
MESH = pl.DeviceIdType.MESH
G = 3
T2 = 16
ROWS = 24


def loop(lo, hi, step, body, init=()):
    count = (hi - lo) // step

    def several(i, carry):
        for j in range(step):
            carry = body(lo + i * step + j, carry)
        return carry

    carry = lax.fori_loop(0, count, several, init)
    for x in range(lo + count * step, hi):
        carry = body(x, carry)
    return carry


def kernel(
    n_p, n_q, b_hbm, k_hbm, s_hbm, g_hbm, m_hbm, sol_hbm, res_hbm,
    K, S, B, Z1, Z2, W, U, V, EX, NY, SY, AZ, BZ, INV, D, Y2,
    geneo, minv, face_lo, face_hi, edge_p, edge_m,
    zs1, zr1, zs2, zr2, ws, wr, cs, cr,
    rc_out, rc1, rc2, c_scr, row_out, ar1, ar2, sol, res,
    load_sem, send_sem, recv_sem, all_sem,
):
    p = lax.axis_index("grp")
    q = lax.axis_index("col")
    nx = k_hbm.shape[0]
    nc = geneo.shape[0]
    ncs = minv.shape[1]
    n_all = n_p * n_q
    me = p * n_q + q
    last = G + nx
    own = pl.ds(G, nx)
    low = pl.ds(0, T2)
    f = slice(None)

    loads = []
    for i, (src, dst) in enumerate((
        (k_hbm, K.at[own, low]), (s_hbm, S.at[own, low]), (b_hbm, B.at[own, low]),
        (g_hbm, geneo), (m_hbm, minv),
    )):
        copy = pltpu.make_async_copy(src, dst, load_sem.at[i])
        copy.start()
        loads.append(copy)

    barrier = pltpu.get_barrier_semaphore()

    def other(t):
        dest = lax.rem(me + t, n_all)
        return (lax.div(dest, n_q), lax.rem(dest, n_q))

    def greet(t, carry):
        pl.semaphore_signal(barrier, inc=1, device_id=other(t), device_id_type=MESH)
        return carry

    lax.fori_loop(1, n_all, greet, 0)

    lane = lax.broadcasted_iota(jnp.int32, (1, 128), 1)
    sub = lax.broadcasted_iota(jnp.int32, (8, 128), 0)
    row = lax.broadcasted_iota(jnp.int32, (ROWS, 128), 0)

    counter = [0]

    def transfer(src, dst, dp, dq):
        i = counter[0]
        counter[0] += 1
        to_p, to_q = p + dp, q + dq
        from_p, from_q = p - dp, q - dq
        sends = (to_p >= 0) & (to_p < n_p) & (to_q >= 0) & (to_q < n_q)
        takes = (from_p >= 0) & (from_p < n_p) & (from_q >= 0) & (from_q < n_q)
        copy = pltpu.make_async_remote_copy(
            src_ref=src, dst_ref=dst, send_sem=send_sem.at[i], recv_sem=recv_sem.at[i],
            device_id=(to_p, to_q), device_id_type=MESH,
        )
        return copy, sends, takes, dst

    pending = []

    def start(items):
        for copy, sends, takes, dst in items:
            pl.when(sends)(copy.start)
            pending.append((copy, sends))

    def arrive(items):
        for copy, sends, takes, dst in items:
            pl.when(takes)(copy.wait_recv)

    def blank(items):
        for copy, sends, takes, dst in items:
            @pl.when(jnp.logical_not(takes))
            def _():
                dst[...] = jnp.zeros(dst.shape, F32)

    r1 = []
    for array, src, width in ((K, k_hbm, 3), (S, s_hbm, 2), (B, b_hbm, 2)):
        r1.append(transfer(src.at[pl.ds(nx - width, width)], array.at[pl.ds(G - width, width), low], 1, 0))
        r1.append(transfer(src.at[pl.ds(0, width)], array.at[pl.ds(last, width), low], -1, 0))
    r1.append(transfer(face_hi, edge_m.at[own], 0, 1))
    r1.append(transfer(face_lo, edge_p.at[own], 0, -1))
    for dp, here, there in ((1, pl.ds(nx - G, G), pl.ds(0, G)), (-1, pl.ds(0, G), pl.ds(last, G))):
        r1.append(transfer(face_hi.at[here], edge_m.at[there], dp, 1))
        r1.append(transfer(face_lo.at[here], edge_p.at[there], dp, -1))

    def z_round(Z, zs, zr):
        return [
            transfer(Z.at[last - 1, low], Z.at[G - 1, low], 1, 0),
            transfer(Z.at[G, low], Z.at[last, low], -1, 0),
            transfer(zs.at[1], zr.at[1], 0, 1),
            transfer(zs.at[0], zr.at[0], 0, -1),
        ]

    r2 = z_round(Z1, zs1, zr1)
    r4 = z_round(Z2, zs2, zr2)
    r3 = [
        transfer(W.at[pl.ds(last - 2, 2), low], W.at[pl.ds(G - 2, 2), low], 1, 0),
        transfer(W.at[pl.ds(G, 2), low], W.at[pl.ds(last, 2), low], -1, 0),
        transfer(ws.at[1], wr.at[1], 0, 1),
        transfer(ws.at[0], wr.at[0], 0, -1),
        transfer(cs.at[0], cr.at[0], 1, 1),
        transfer(cs.at[1], cr.at[1], 1, -1),
        transfer(cs.at[2], cr.at[2], -1, 1),
        transfer(cs.at[3], cr.at[3], -1, -1),
    ]
    for items in (r1, r2, r3, r4):
        blank(items)

    def clear(x, carry):
        for Z in (Z1, Z2):
            Z[x, 16:24] = jnp.zeros((8, 128), F32)
        return carry

    loop(G, last, 16, clear)

    def spread(src, dst, i, devices):
        count, slot, where = devices

        def one(t):
            return pltpu.make_async_remote_copy(
                src_ref=src, dst_ref=dst.at[slot], send_sem=all_sem.at[2 * i], recv_sem=all_sem.at[2 * i + 1],
                device_id=where(t), device_id_type=MESH,
            )

        def go(t, carry):
            one(t).start()
            return carry

        lax.fori_loop(1, count, go, 0)
        dst[slot] = src[...]

        def whole():
            part = dst.at[pl.ds(0, count - 1)]
            return pltpu.make_async_remote_copy(
                src_ref=part, dst_ref=part, send_sem=all_sem.at[2 * i], recv_sem=all_sem.at[2 * i + 1],
                device_id=where(1), device_id_type=MESH,
            )

        return whole

    in_col = (n_q, q, lambda t: (p, lax.rem(q + t, n_q)))
    in_all = (n_all, me, other)

    def packed(parts, first_lane):
        tile = jnp.zeros((8, 128), F32)
        for i, part in enumerate(parts):
            tile = jnp.where(sub == i, jnp.sum(part, axis=0, keepdims=True), tile)
        sums = jnp.sum(tile, axis=1, keepdims=True)
        lanes = lax.broadcasted_iota(jnp.int32, (8, 128), 1)
        placed = jnp.where(lanes == sub + first_lane, sums, 0.0)
        return jnp.sum(jnp.where(sub < len(parts), placed, 0.0), axis=0, keepdims=True)

    def restrict(src):
        def step(x, carry):
            value = src[x, low]
            return tuple(acc + geneo[j, x - G].astype(F32) * value for j, acc in enumerate(carry))

        sums = loop(G, last, 16, step, tuple(jnp.zeros((T2, 128), F32) for _ in range(nc)))
        return packed(sums, q * nc)

    def coarse(rc):
        total = rc[0]
        for i in range(1, n_q):
            total = total + rc[i]
        c = jnp.sum(minv[0] * total[:, :ncs], axis=1, keepdims=True)
        c_scr[...] = jnp.broadcast_to(c, (ncs, 128))
        return [c_scr[pl.ds(q * nc + j, 1), :] for j in range(nc)]

    for copy in loads[:3]:
        copy.wait()

    def pack(x, carry):
        kl, sl, bl = K[x, 0:8], S[x, 0:8], B[x, 0:8]
        kt, st, bt = K[x, 8:16], S[x, 8:16], B[x, 8:16]
        face_lo[x - G] = jnp.where(sub < 3, kl, jnp.where(sub < 5, pltpu.roll(sl, 3, 0), pltpu.roll(bl, 5, 0)))
        face_hi[x - G] = jnp.where(sub > 4, kt, jnp.where(sub > 2, pltpu.roll(st, 5, 0), pltpu.roll(bt, 3, 0)))
        return carry

    loop(G, last, 4, pack)
    pl.semaphore_wait(barrier, n_all - 1)
    start(r1)
    loads[3].wait()
    loads[4].wait()
    rc_out[0] = restrict(B)
    rc_wait1 = spread(rc_out.at[0], rc1, 0, in_col)
    arrive(r1)

    def fill(x, carry):
        plus, minus = edge_p[x], edge_m[x]
        K[x, 16:24] = jnp.where(sub < 4, plus, minus)
        S[x, 16:24] = jnp.where(sub < 4, pltpu.roll(plus, 5, 0), pltpu.roll(minus, 3, 0))
        B[x, 16:24] = jnp.where(sub < 4, pltpu.roll(plus, 3, 0), pltpu.roll(minus, 5, 0))
        return carry

    loop(0, last + G, 16, fill)
    y_ok = (row < T2) | ((row < T2 + 2) & (q < n_q - 1)) | ((row >= ROWS - 2) & (q > 0))

    EX[0] = 0.5 * (K[0] + K[1])

    def terms(x, carry):
        kh = 0.5 * K[x]
        east = kh + 0.5 * K[x + 1]
        EX[x] = east
        north = kh + pltpu.roll(kh, ROWS - 1, 0)
        south = kh + pltpu.roll(kh, 1, 0)
        above = jnp.where(lane < 127, pltpu.roll(kh, 127, 1), 0.0)
        below = jnp.where(lane > 0, pltpu.roll(kh, 1, 1), 0.0)
        d = S[x] + east + EX[x - 1] + north + south + ((kh + above) + (kh + below))
        x_ok = ((x >= G) | (p > 0)) & ((x < last) | (p < n_p - 1))
        inv = jnp.where(y_ok & x_ok, 1.0 / d, 0.0)
        NY[x] = north
        SY[x] = south
        AZ[x] = jnp.where(lane < 127, kh + above, 0.0)
        BZ[x] = jnp.where(lane > 0, kh + below, 0.0)
        D[x] = d
        INV[x] = inv
        U[x] = inv * B[x]
        return carry

    loop(1, last + 2, 16, terms)

    def beside(A, x, r):
        mid = A[x]
        total = EX[x - 1, r] * A[x - 1, r] + EX[x, r] * A[x + 1, r]
        total = total + NY[x, r] * pltpu.roll(mid, ROWS - 1, 0)[r] + SY[x, r] * pltpu.roll(mid, 1, 0)[r]
        part = mid[r]
        return total + AZ[x, r] * pltpu.roll(part, 127, 1) + BZ[x, r] * pltpu.roll(part, 1, 1)

    every = slice(0, ROWS)
    mine = slice(0, T2)

    def solve(src, dst, rc, zs, faces):
        def second(x, carry):
            V[x] = INV[x] * (src[x] + beside(U, x, every))
            return carry

        loop(G - 1, last + 1, 16, second)
        c = coarse(rc)

        def third(x, carry):
            value = INV[x, mine] * (src[x, mine] + beside(V, x, mine))
            for j in range(nc):
                value = value + c[j] * geneo[j, x - G].astype(F32)
            dst[x, mine] = value
            zs[0, pl.ds(x - G, 1)] = value[0:1]
            zs[1, pl.ds(x - G, 1)] = value[15:16]
            return carry

        third(G, ())
        third(last - 1, ())
        start(faces[:2])
        loop(G + 1, last - 1, 15, third)
        start(faces[2:])

    def image(Z, put, faces):
        def step(x, carry):
            put(x, D[x, mine] * Z[x, mine] - beside(Z, x, mine))
            return carry

        loop(G + 1, last - 1, 15, step)
        arrive(faces)
        step(G, ())
        step(last - 1, ())

    def with_faces(value, x, zr):
        i = pl.ds(x - G, 1)
        top = jnp.where(sub == 0, SY[x, 0:8] * zr[1, i], 0.0)
        bottom = jnp.where(sub == 7, NY[x, 8:16] * zr[0, i], 0.0)
        return value - jnp.concatenate([top, bottom], axis=0)

    rc_wait1().wait_recv()
    solve(B, Z1, rc1, zs1, r2)

    def put_one(x, value):
        W[x, mine] = value

    image(Z1, put_one, r2)

    zero = jnp.zeros((T2, 128), F32)

    def image_one(x, carry):
        bb, bw, ww = carry
        w = with_faces(W[x, mine], x, zr1)
        b = B[x, mine]
        W[x, mine] = w
        i = x - G
        ws[0, pl.ds(i, 1)] = w[0:1]
        ws[0, pl.ds(nx + i, 1)] = w[1:2]
        ws[1, pl.ds(i, 1)] = w[15:16]
        ws[1, pl.ds(nx + i, 1)] = w[14:15]
        return bb + b * b, bw + b * w, ww + w * w

    bb_part, bw_part, ww_part = loop(G, last, 16, image_one, (zero, zero, zero))
    for i, (x, r) in enumerate(((last - 1, 15), (last - 1, 0), (G, 15), (G, 0))):
        cs[i] = jnp.broadcast_to(W[x, r : r + 1], (8, 128))
    start(r3)
    rc_out[1] = restrict(W)
    rc_wait2 = spread(rc_out.at[1], rc2, 1, in_col)
    row_out[0] = packed((bb_part, bw_part, ww_part), 0)
    ar_wait1 = spread(row_out.at[0], ar1, 2, in_all)
    arrive(r3)

    def put_w(x, carry):
        i = x - G
        tile = jnp.where(sub == 0, wr[0, pl.ds(i, 1)], jnp.where(sub == 1, wr[0, pl.ds(nx + i, 1)], 0.0))
        tile = jnp.where(sub == 7, wr[1, pl.ds(i, 1)], jnp.where(sub == 6, wr[1, pl.ds(nx + i, 1)], tile))
        W[x, 16:24] = tile
        return carry

    loop(G, last, 16, put_w)
    blank_tile = jnp.zeros((8, 128), F32)
    W[G - 2, 16:24] = blank_tile
    W[last + 1, 16:24] = blank_tile
    W[G - 1, 16:24] = jnp.where(sub == 7, cr[0], jnp.where(sub == 0, cr[1], 0.0))
    W[last, 16:24] = jnp.where(sub == 7, cr[2], jnp.where(sub == 0, cr[3], 0.0))

    def first_sweep(x, carry):
        U[x] = INV[x] * W[x]
        return carry

    loop(G - 2, last + 2, 16, first_sweep)
    rc_wait2().wait_recv()
    solve(W, Z2, rc2, zs2, r4)

    def totals(ar):
        if n_all <= 64:
            total = ar[0]
            for i in range(1, n_all):
                total = total + ar[i]
        else:
            total = lax.fori_loop(1, n_all, lambda i, acc: acc + ar[i], ar[0])
        return [jnp.sum(jnp.where(lane == i, total, 0.0), axis=1, keepdims=True) for i in range(3)]


    def put_two(x, value):
        Y2[x - G] = value

    image(Z2, put_two, r4)
    ar_wait1().wait_recv()
    bb, bw, ww = totals(ar1)
    h = bw / bb

    def image_two(x, carry):
        wq, qq, bq = carry
        w = W[x, mine]
        value = with_faces(Y2[x - G], x, zr2) - h * w
        Y2[x - G] = value
        return wq + w * value, qq + value * value, bq + B[x, mine] * value

    wq_part, qq_part, bq_part = loop(G, last, 16, image_two, (zero, zero, zero))
    row_out[1] = packed((wq_part, qq_part, bq_part), 0)
    ar_wait2 = spread(row_out.at[1], ar2, 3, in_all)
    ar_wait2().wait_recv()
    wq, qq, bq = totals(ar2)
    g11, g12, g22 = ww / bb, wq / bb, qq / bb
    rhs_one, rhs_two = h, bq / bb
    determinant = g11 * g22 - g12 * g12
    y_one = (g22 * rhs_one - g12 * rhs_two) / determinant
    y_two = (g11 * rhs_two - g12 * rhs_one) / determinant
    y_mix = y_one - y_two * h

    def finish(x, carry):
        sol[x - G] = y_mix * Z1[x, mine] + y_two * Z2[x, mine]
        res[x - G] = B[x, mine] - y_one * W[x, mine] - y_two * Y2[x - G]
        return carry

    loop(G, last, 4, finish)
    outs = []
    for i, (src, dst) in enumerate(((sol, sol_hbm), (res, res_hbm))):
        copy = pltpu.make_async_copy(src, dst, load_sem.at[5 + i])
        copy.start()
        outs.append(copy)
    for copy, sends in pending:
        pl.when(sends)(copy.wait_send)
    for wait in (rc_wait1, rc_wait2, ar_wait1, ar_wait2):
        wait().wait_send()
    for copy in outs:
        copy.wait()


def body(n_p, n_q, right_side, conductance, reaction, geneo, coarse_inverse):
    nx, ny, nz = right_side.shape
    assert ny == T2 and nz == 128
    nc = geneo.shape[0]
    ncs = coarse_inverse.shape[1]
    n_all = n_p * n_q
    region = pltpu.VMEM((nx + 2 * G, ROWS, nz), F32)
    field = pltpu.VMEM((nx, ny, nz), F32)
    scratch = [region] * 15 + [
        field,
        pltpu.VMEM(geneo.shape, geneo.dtype),
        pltpu.VMEM(coarse_inverse.shape, F32),
        pltpu.VMEM((nx, 8, nz), F32), pltpu.VMEM((nx, 8, nz), F32),
        pltpu.VMEM((nx + 2 * G, 8, nz), F32), pltpu.VMEM((nx + 2 * G, 8, nz), F32),
    ]
    scratch += [pltpu.VMEM((2, nx, nz), F32)] * 4
    scratch += [pltpu.VMEM((2, 2 * nx, nz), F32)] * 2
    scratch += [pltpu.VMEM((4, 8, nz), F32)] * 2
    scratch += [
        pltpu.VMEM((2, 1, nz), F32), pltpu.VMEM((n_q, 1, nz), F32), pltpu.VMEM((n_q, 1, nz), F32),
        pltpu.VMEM((ncs, nz), F32),
        pltpu.VMEM((2, 1, nz), F32), pltpu.VMEM((n_all, 1, nz), F32), pltpu.VMEM((n_all, 1, nz), F32),
        field, field,
        pltpu.SemaphoreType.DMA((7,)),
        pltpu.SemaphoreType.DMA((28,)), pltpu.SemaphoreType.DMA((28,)),
        pltpu.SemaphoreType.DMA((8,)),
    ]
    out = jax.ShapeDtypeStruct(right_side.shape, F32)
    return pl.pallas_call(
        functools.partial(kernel, n_p, n_q),
        out_shape=(out, out),
        in_specs=[pl.BlockSpec(memory_space=pl.ANY)] * 5,
        out_specs=(pl.BlockSpec(memory_space=pl.ANY),) * 2,
        scratch_shapes=scratch,
        compiler_params=pltpu.CompilerParams(collective_id=0, has_side_effects=True, vmem_limit_bytes=67043328),
    )(right_side, conductance, reaction, geneo, coarse_inverse)


def solution(mesh):
    return jax.shard_map(
        functools.partial(body, mesh.shape["grp"], mesh.shape["col"]),
        mesh=mesh,
        in_specs=(
            P("grp", "col", None),
            P("grp", "col", None),
            P("grp", "col", None),
            P(None, "grp", "col", None),
            P("grp", None, None),
        ),
        out_specs=(P("grp", "col", None), P("grp", "col", None)),
        check_vma=False,
    )
```
